768 devices in a mesh: blk: 24 (over z, y_hi), section: 32 (over y_lo, x, core).
Axes of the slice: x: 4, y: 8 (y_hi: 2, y_lo: 4; y = y_hi * 4 + y_lo), z: 12, core: 2. Of those that a mesh axis runs over, the one named last changes fastest.
Arguments:
- text_emb: bfloat16 [32, 6144, 1024], P(None, ('blk', 'section')), may hold values from -6 to 6
- covariate: bfloat16 [32, 1536, 1024], P('section', 'blk'), may hold values from -6 to 6
- labels: int32 [32, 6144], P('section', 'blk'), may hold values from 0 to 1535, as said below
- logit_scale: float32 [1], replicated, may hold values from 0.02 to 0.08
- logit_bias: float32 [1], replicated, may hold values from -3 to -1
Outputs:
- text_grad: float32 [32, 6144, 1024], P('section', 'blk')
- cov_grad: float32 [32, 1536, 1024], P('section', 'blk')
The draws below stay inside these ranges and needn't reach their ends.
Inputs may be any that keep to these rules, and one draw needn't show every extreme that they name: `labels`: every covariate row of a group is the positive of exactly 4 text rows of that group.
All inputs are finite; a program needn't handle non-finite values.
Results may differ from the reference program's by a relative error of at most 0.0025.
Values may be sent and summed in bfloat16 or wider, within the bound.
A program may use at most 32 MiB of HBM per device.

```python
import math
import jax
import jax.numpy as jnp
from jax import lax

D = 1024
COV_DEV = 64
TXT_GROUP = 6144
COV_GROUP = 1536
N_BLK = 24
N_SECTION = 32


def draw_labels(key, part):
    group_keys = jax.random.split(key, N_SECTION)
    orders = jax.vmap(lambda one_key: jax.random.permutation(one_key, TXT_GROUP))(group_keys)
    return (orders.astype(jnp.int32) % COV_GROUP).astype(jnp.int32)


def shard_levels(own_key, dims, cuts, least, high):
    level, own = 1.0, jax.random.fold_in(own_key, 6)
    for axis_at, parts in cuts:
        draws = jnp.exp(jax.random.uniform(jax.random.fold_in(own, axis_at), (parts,), jnp.float32, least / len(cuts), high / len(cuts)))
        level = level * jnp.repeat(draws, dims[axis_at] // parts).reshape([-1 if axis == axis_at else 1 for axis in range(len(dims))])
    return level


def noise(rng, shape, scale, limit, shards=(), kind=jnp.bfloat16):
    gain = shard_levels(rng, shape, shards, -0.22, 0.18) if shards else 1.0
    result = jax.random.normal(rng, shape, jnp.float32) * scale * gain
    return jnp.minimum(jnp.maximum(result, -limit), limit).astype(kind)


def setup_inputs(seed: int = 0) -> dict:
    key_of = jax.random.split(jax.random.key(seed), 6)
    return {
        "text_emb": noise(key_of[0], (N_SECTION, TXT_GROUP, D), 1.0, 6.0, ((1, 768),)),
        "covariate": noise(key_of[1], (N_SECTION, COV_GROUP, D), 1.0, 6.0, ((0, 32), (1, 24))),
        "labels": draw_labels(jax.random.fold_in(key_of[5], 71), 0),
        "logit_scale": jnp.clip(jnp.exp(jax.random.uniform(key_of[3], (1,), jnp.float32, math.log(0.02), math.log(0.08))), 0.02, 0.08),
        "logit_bias": jnp.clip(jax.random.uniform(key_of[4], (1,), jnp.float32, -3.0, -1.0), -3.0, -1.0),
    }


def reference(text_emb, covariate, labels, logit_scale, logit_bias):
    factor = logit_scale[0]
    offset = logit_bias[0]
    block_ids = jnp.arange(COV_GROUP, dtype=jnp.int32).reshape(N_BLK, COV_DEV)

    def one_group(group_in):
        text_rows, cov_rows, group_labels = group_in
        cov_blocks = cov_rows.reshape(N_BLK, COV_DEV, D)

        def block_step(text_acc, blocks_in):
            cov_block, row_ids = blocks_in
            logits = factor * jnp.dot(cov_block, text_rows.T, preferred_element_type=jnp.float32) + offset
            positive = (group_labels[None, :] == row_ids[:, None]).astype(jnp.float32)
            weights_bf = (factor * (jax.nn.sigmoid(logits) - positive)).astype(jnp.bfloat16)
            cov_term = jnp.dot(weights_bf, text_rows, preferred_element_type=jnp.float32)
            text_acc = text_acc + jnp.dot(weights_bf.T, cov_block, preferred_element_type=jnp.float32)
            return text_acc, cov_term

        start_acc = jnp.zeros((TXT_GROUP, D), jnp.float32)
        text_part, cov_terms = lax.scan(block_step, start_acc, (cov_blocks, block_ids))
        return text_part, cov_terms.reshape(COV_GROUP, D)

    text_grad, cov_grad = lax.map(one_group, (text_emb, covariate, labels))
    return text_grad, cov_grad
```

```python
import functools

import jax
import jax.numpy as jnp
from jax import lax
from jax.experimental import pallas as pl
from jax.experimental.pallas import tpu as pltpu
from jax.sharding import PartitionSpec as P

MESH = pl.DeviceIdType.MESH
F32 = jnp.float32
BF16 = jnp.bfloat16
PIECES = 4
Y_LO = 4


def kernel(
    dims,
    panel_ref, cov_ref, lab_ref, scale_ref, bias_ref,
    text_out, cov_out,
    cov_all, lab_far, weights, cov_part,
    rs_out, rs_in, last_out, last_in, tx_out, tx_mid, tx_in,
    ag_send, ag_recv, rs_send, rs_recv, t1_send, t1_recv, t2_send, t2_recv, lab_sem, own_sem,
):
    n_z, y_lo, per_y = dims
    reach = n_z // 2
    rows_dev, width = cov_ref.shape
    half_rows = rows_dev // 2
    blk, sec = lax.axis_index("blk"), lax.axis_index("section")
    z, y_hi = blk // 2, blk % 2
    y, rest = y_hi * y_lo + sec // per_y, sec % per_y

    def at_z(step):
        return {"blk": ((z + step + n_z) % n_z) * 2 + y_hi, "section": sec}

    def at_y(step):
        other = (y + step + 2 * y_lo) % (2 * y_lo)
        return {"blk": z * 2 + other // y_lo, "section": (other % y_lo) * per_y + rest}

    z_next = (at_z(1), at_z(-1))
    y_next = (at_y(y_lo // 2), at_y(-(y_lo // 2)))
    far = at_y(y_lo)

    barrier = pltpu.get_barrier_semaphore()
    for peer in (*z_next, *y_next, far):
        pl.semaphore_signal(barrier, inc=1, device_id=peer, device_id_type=MESH)
    pl.semaphore_wait(barrier, 5)

    def remote(src, dst, send, recv, peer):
        return pltpu.make_async_remote_copy(
            src_ref=src, dst_ref=dst, send_sem=send, recv_sem=recv, device_id=peer, device_id_type=MESH
        )

    lab_copy = remote(lab_ref, lab_far, lab_sem.at[0], lab_sem.at[1], far)
    lab_copy.start()

    def hops(way, half):
        return reach - (1 if way == half else 0) if n_z % 2 == 0 else reach

    def slot(way, k):
        return (k if way == 0 else -k) % n_z

    def gather_copy(way, half, k):
        src = cov_ref.at[pl.ds(half * half_rows, half_rows)] if k == 0 else cov_all.at[slot(way, k), half]
        return remote(
            src, cov_all.at[slot(way, k + 1), half],
            ag_send.at[way, half, k], ag_recv.at[way, half, k], z_next[way],
        )

    own_copies = [
        pltpu.make_async_copy(cov_ref.at[pl.ds(half * half_rows, half_rows)], cov_all.at[0, half], own_sem.at[half])
        for half in range(2)
    ]
    for k in range(reach):
        for half in range(2):
            for way in range(2):
                if k >= 1 and k - 1 < hops(way, half):
                    gather_copy(way, half, k - 1).wait_recv()
                if k < hops(way, half):
                    gather_copy(way, half, k).start()
    for copy in own_copies:
        copy.start()
    for copy in own_copies:
        copy.wait()
    for half in range(2):
        for way in range(2):
            if hops(way, half) == reach:
                gather_copy(way, half, reach - 1).wait_recv()
    lab_copy.wait_recv()

    scale, bias = scale_ref[0], bias_ref[0]
    rows_txt = lab_ref.shape[1]
    cov_rows = cov_all[...].reshape(n_z * rows_dev, width)
    row_at = lax.broadcasted_iota(jnp.int32, (rows_dev, rows_txt), 0)

    def panel_of(side):
        n_src = panel_ref.shape[0] // 2
        return panel_ref[pl.ds(side * n_src, n_src)].reshape(rows_txt, width)

    def fill_weights(panel, labels, column):
        logits = lax.dot_general(cov_rows, panel, (((1,), (1,)), ((), ())), preferred_element_type=F32)
        for k in range(n_z):
            part = logits[k * rows_dev : (k + 1) * rows_dev]
            first = (((z - k + n_z) % n_z) * 2 + y_hi) * rows_dev
            positive = (labels - first == row_at).astype(F32)
            value = scale * (jax.nn.sigmoid(scale * part + bias) - positive)
            weights[pl.ds(k * rows_dev, rows_dev), pl.ds(column, rows_txt)] = value.astype(BF16)

    def text_term(column):
        return lax.dot_general(
            weights[:, pl.ds(column, rows_txt)], cov_rows, (((0,), (0,)), ((), ())), preferred_element_type=F32
        )

    panel_far = panel_of(1 - y_hi)
    fill_weights(panel_far, lab_far[...], rows_txt)
    piece = rows_txt // (2 * PIECES)
    tx_out[...] = text_term(rows_txt).astype(BF16).reshape(2, PIECES, piece, width)

    def first_leg(way, j):
        return remote(
            tx_out.at[way, j], tx_mid.at[way, j], t1_send.at[way, j], t1_recv.at[way, j], y_next[way]
        )

    def second_leg(way, j):
        return remote(
            tx_mid.at[way, j], tx_in.at[way, j], t2_send.at[way, j], t2_recv.at[way, j], y_next[way]
        )

    for j in range(PIECES):
        for way in range(2):
            first_leg(way, j).start()

    panel_own = panel_of(y_hi)
    fill_weights(panel_own, lab_ref[...], 0)
    cov_part[...] = (
        jnp.dot(weights[:, pl.ds(0, rows_txt)], panel_own, preferred_element_type=F32)
        + jnp.dot(weights[:, pl.ds(rows_txt, rows_txt)], panel_far, preferred_element_type=F32)
    ).reshape(n_z, 2, half_rows, width)

    def part_of(way, half, m):
        return cov_part[(-m if way == 0 else m) % n_z, half]

    def sum_copy(way, half, m):
        src = last_out.at[way, half] if m == 1 else rs_out.at[way, half, m - 1]
        dst = last_in.at[way, half] if m == 1 else rs_in.at[way, half, m - 1]
        return remote(
            src, dst,
            rs_send.at[way, half, m - 1], rs_recv.at[way, half, m - 1], z_next[way],
        )

    def sum_start(way, half, m):
        total = part_of(way, half, m)
        if m < hops(way, half):
            sum_copy(way, half, m + 1).wait_recv()
            total = total + rs_in[way, half, m].astype(F32)
        if m == 1:
            last_out[way, half] = total
        else:
            rs_out[way, half, m - 1] = total.astype(BF16)
        sum_copy(way, half, m).start()

    for half in range(2):
        for way in range(2):
            sum_start(way, half, hops(way, half))
    text_out[...] = text_term(0)

    forwarded = 0
    for step in range(1, reach):
        if forwarded < PIECES:
            for way in range(2):
                first_leg(way, forwarded).wait_recv()
                second_leg(way, forwarded).start()
            forwarded += 1
        for half in range(2):
            for way in range(2):
                m = hops(way, half) - step
                if m >= 1:
                    sum_start(way, half, m)
    while forwarded < PIECES:
        for way in range(2):
            first_leg(way, forwarded).wait_recv()
            second_leg(way, forwarded).start()
        forwarded += 1

    for half in range(2):
        total = cov_part[0, half]
        for way in range(2):
            sum_copy(way, half, 1).wait_recv()
            total = total + last_in[way, half]
        cov_out[pl.ds(half * half_rows, half_rows)] = total

    for j in range(PIECES):
        for way in range(2):
            second_leg(way, j).wait_recv()
            rows = pl.ds((way * PIECES + j) * piece, piece)
            text_out[rows] = text_out[rows] + tx_in[way, j].astype(F32)

    lab_copy.wait_send()
    for half in range(2):
        for way in range(2):
            for k in range(hops(way, half)):
                gather_copy(way, half, k).wait_send()
                sum_copy(way, half, k + 1).wait_send()
    for j in range(PIECES):
        for way in range(2):
            first_leg(way, j).wait_send()
            second_leg(way, j).wait_send()


def local(dims, text_emb, covariate, labels, logit_scale, logit_bias):
    n_z, y_lo, per_y = dims
    sections = y_lo * per_y
    plane = 2 * sections
    groups = [[at * plane + i for i in range(plane)] for at in range(n_z)]
    panel = lax.all_to_all(
        jnp.concatenate([text_emb, text_emb], 0), ("blk", "section"),
        split_axis=0, concat_axis=0, tiled=True, axis_index_groups=groups,
    )
    cov_own = covariate[0]
    rows_dev, width = cov_own.shape
    rows_txt = labels.shape[1]
    piece = rows_txt // (2 * PIECES)
    reach = n_z // 2
    half_rows = rows_dev // 2
    dma = pltpu.SemaphoreType.DMA
    vmem = pl.BlockSpec(memory_space=pltpu.VMEM)
    smem = pl.BlockSpec(memory_space=pltpu.SMEM)
    text_grad, cov_grad = pl.pallas_call(
        functools.partial(kernel, dims),
        out_shape=(
            jax.ShapeDtypeStruct((rows_txt, width), F32),
            jax.ShapeDtypeStruct((rows_dev, width), F32),
        ),
        in_specs=[vmem, vmem, vmem, smem, smem],
        out_specs=(vmem, vmem),
        scratch_shapes=[
            pltpu.VMEM((n_z, 2, half_rows, width), BF16),
            pltpu.VMEM((1, rows_txt), jnp.int32),
            pltpu.VMEM((n_z * rows_dev, 2 * rows_txt), BF16),
            pltpu.VMEM((n_z, 2, half_rows, width), F32),
            pltpu.VMEM((2, 2, reach, half_rows, width), BF16),
            pltpu.VMEM((2, 2, reach, half_rows, width), BF16),
            pltpu.VMEM((2, 2, half_rows, width), F32),
            pltpu.VMEM((2, 2, half_rows, width), F32),
            pltpu.VMEM((2, PIECES, piece, width), BF16),
            pltpu.VMEM((2, PIECES, piece, width), BF16),
            pltpu.VMEM((2, PIECES, piece, width), BF16),
            dma((2, 2, reach)), dma((2, 2, reach)), dma((2, 2, reach)), dma((2, 2, reach)),
            dma((2, PIECES)), dma((2, PIECES)), dma((2, PIECES)), dma((2, PIECES)),
            dma((2,)), dma((2,)),
        ],
        compiler_params=pltpu.CompilerParams(
            collective_id=0, has_side_effects=True, vmem_limit_bytes=48 * 1024 * 1024
        ),
    )(panel, cov_own, labels, logit_scale, logit_bias)
    return text_grad[None], cov_grad[None]


def solution(mesh):
    dims = (mesh.shape["blk"] // 2, Y_LO, mesh.shape["section"] // Y_LO)
    return jax.shard_map(
        functools.partial(local, dims),
        mesh=mesh,
        in_specs=(
            P(None, ("blk", "section"), None),
            P("section", "blk", None),
            P("section", "blk"),
            P(),
            P(),
        ),
        out_specs=(P("section", "blk", None), P("section", "blk", None)),
        check_vma=False,
    )
```

```python
import functools

import jax
import jax.numpy as jnp
from jax import lax
from jax.experimental import pallas as pl
from jax.experimental.pallas import tpu as pltpu
from jax.sharding import PartitionSpec as P

MESH = pl.DeviceIdType.MESH
F32 = jnp.float32
BF16 = jnp.bfloat16
PIECES = 8
TIE_RELAY = True
Y_LO = 4


def kernel(
    dims,
    text_ref, cov_ref, lab_ref, scale_ref, bias_ref,
    text_out, cov_out,
    panel, tie_buf, cov_all, lab_far, weights, cov_part,
    rs_out, rs_in, last_out, last_in, tx_out, tx_mid, tx_in,
    ag_send, ag_recv, rs_send, rs_recv, t1_send, t1_recv, t2_send, t2_recv, lab_sem, own_sem,
    near_sem, far_sem, tie_send, tie_recv, tie_out,
):
    n_z, y_lo, per_y = dims
    reach = n_z // 2
    rows_dev, width = cov_ref.shape
    half_rows = rows_dev // 2
    blk, sec = lax.axis_index("blk"), lax.axis_index("section")
    z, y_hi = blk // 2, blk % 2
    y, rest = y_hi * y_lo + sec // per_y, sec % per_y

    def at_z(step):
        return {"blk": ((z + step + n_z) % n_z) * 2 + y_hi, "section": sec}

    def at_y(step):
        other = (y + step + 2 * y_lo) % (2 * y_lo)
        return {"blk": z * 2 + other // y_lo, "section": (other % y_lo) * per_y + rest}

    z_next = (at_z(1), at_z(-1))
    y_next = (at_y(y_lo // 2), at_y(-(y_lo // 2)))
    far = at_y(y_lo)

    sections = y_lo * per_y
    plane = 2 * sections
    barrier = pltpu.get_barrier_semaphore()
    for peer in z_next:
        pl.semaphore_signal(barrier, inc=1, device_id=peer, device_id_type=MESH)

    @pl.loop(1, plane)
    def _(step):
        other = (y_hi * sections + sec + step) % plane
        peer = {"blk": z * 2 + other // sections, "section": other % sections}
        pl.semaphore_signal(barrier, inc=1, device_id=peer, device_id_type=MESH)

    pl.semaphore_wait(barrier, plane + 1)

    def remote(src, dst, send, recv, peer):
        return pltpu.make_async_remote_copy(
            src_ref=src, dst_ref=dst, send_sem=send, recv_sem=recv, device_id=peer, device_id_type=MESH
        )

    near_send, near_recv, far_send, far_recv = near_sem.at[0], near_sem.at[1], far_sem.at[0], far_sem.at[1]
    half_y = per_y // 2
    y_own = sec // per_y

    def tie_copy(way):
        return remote(
            text_ref.at[pl.ds(y_own * per_y + way * half_y, half_y)], tie_buf.at[way],
            tie_send.at[way], tie_recv.at[way], y_next[way],
        )

    def tie_onward(way):
        y_from = (y + (-1 if way == 0 else 1) * (y_lo // 2) + 2 * y_lo) % (2 * y_lo)
        y_to = (y + (1 if way == 0 else -1) * (y_lo // 2) + 2 * y_lo) % (2 * y_lo)
        origin = (y_from % y_lo) * per_y + rest

        @pl.loop(0, half_y)
        def _(i):
            peer = {"blk": z * 2 + y_to // y_lo, "section": (y_to % y_lo) * per_y + way * half_y + i}
            remote(tie_buf.at[way, i], panel.at[1, origin], tie_out.at[way], far_recv, peer).start()

    if TIE_RELAY:
        for way in range(2):
            tie_copy(way).start()

    @pl.loop(0, per_y)
    def _(step):
        column = (rest + step) % per_y
        for dy in range(1 if TIE_RELAY else 0, y_lo):
            to = ((y_own + dy) % y_lo) * per_y + column
            peer = {"blk": z * 2 + 1 - y_hi, "section": to}
            remote(text_ref.at[to], panel.at[1, sec], far_send, far_recv, peer).start()

    lab_copy = remote(lab_ref, lab_far, lab_sem.at[0], lab_sem.at[1], far)
    lab_copy.start()

    def hops(way, half):
        return reach - (1 if way == half else 0) if n_z % 2 == 0 else reach

    def slot(way, k):
        return (k if way == 0 else -k) % n_z

    def gather_copy(way, half, k):
        src = cov_ref.at[pl.ds(half * half_rows, half_rows)] if k == 0 else cov_all.at[slot(way, k), half]
        return remote(
            src, cov_all.at[slot(way, k + 1), half],
            ag_send.at[way, half, k], ag_recv.at[way, half, k], z_next[way],
        )

    own_copies = [
        pltpu.make_async_copy(cov_ref.at[pl.ds(half * half_rows, half_rows)], cov_all.at[0, half], own_sem.at[half])
        for half in range(2)
    ]
    for k in range(reach):
        if k == 1:

            @pl.loop(0, per_y)
            def _(step):
                column = (rest + step) % per_y
                for dy in range(1, y_lo):
                    to = ((y_own + dy) % y_lo) * per_y + column
                    peer = {"blk": blk, "section": to}
                    remote(text_ref.at[to], panel.at[0, sec], near_send, near_recv, peer).start()

            @pl.loop(1, per_y)
            def _(step):
                to = y_own * per_y + (rest + step) % per_y
                peer = {"blk": blk, "section": to}
                remote(text_ref.at[to], panel.at[0, sec], near_send, near_recv, peer).start()

            pltpu.make_async_copy(text_ref.at[sec], panel.at[0, sec], near_recv).start()
        if k == min(2, reach - 1) and TIE_RELAY:
            for way in range(2):
                tie_copy(way).wait_recv()
                tie_onward(way)
        for half in range(2):
            for way in range(2):
                if k >= 1 and k - 1 < hops(way, half):
                    gather_copy(way, half, k - 1).wait_recv()
                if k < hops(way, half):
                    gather_copy(way, half, k).start()
    for copy in own_copies:
        copy.start()
    for copy in own_copies:
        copy.wait()
    for half in range(2):
        for way in range(2):
            if hops(way, half) == reach:
                gather_copy(way, half, reach - 1).wait_recv()
    lab_copy.wait_recv()

    scale, bias = scale_ref[0], bias_ref[0]
    rows_txt = lab_ref.shape[1]
    cov_rows = cov_all[...].reshape(n_z * rows_dev, width)
    row_at = lax.broadcasted_iota(jnp.int32, (rows_dev, rows_txt), 0)

    def whole(side, send, recv):
        return remote(panel.at[side], panel.at[side], send, recv, far)

    def fill_weights(panel, labels, column):
        logits = lax.dot_general(cov_rows, panel, (((1,), (1,)), ((), ())), preferred_element_type=F32)
        for k in range(n_z):
            part = logits[k * rows_dev : (k + 1) * rows_dev]
            first = (((z - k + n_z) % n_z) * 2 + y_hi) * rows_dev
            positive = (labels - first == row_at).astype(F32)
            value = scale * (jax.nn.sigmoid(scale * part + bias) - positive)
            weights[pl.ds(k * rows_dev, rows_dev), pl.ds(column, rows_txt)] = value.astype(BF16)

    def text_term(column):
        return lax.dot_general(
            weights[:, pl.ds(column, rows_txt)], cov_rows, (((0,), (0,)), ((), ())), preferred_element_type=F32
        )

    whole(1, far_send, far_recv).wait_recv()
    panel_far = panel[1].reshape(rows_txt, width)
    fill_weights(panel_far, lab_far[...], rows_txt)
    piece = rows_txt // (2 * PIECES)
    tx_out[...] = text_term(rows_txt).astype(BF16).reshape(2, PIECES, piece, width)

    def first_leg(way, j):
        return remote(
            tx_out.at[way, j], tx_mid.at[way, j], t1_send.at[way, j], t1_recv.at[way, j], y_next[way]
        )

    def second_leg(way, j):
        return remote(
            tx_mid.at[way, j], tx_in.at[way, j], t2_send.at[way, j], t2_recv.at[way, j], y_next[way]
        )

    for j in range(PIECES):
        for way in range(2):
            first_leg(way, j).start()

    whole(0, near_send, near_recv).wait_recv()
    panel_own = panel[0].reshape(rows_txt, width)
    fill_weights(panel_own, lab_ref[...], 0)
    cov_part[...] = (
        jnp.dot(weights[:, pl.ds(0, rows_txt)], panel_own, preferred_element_type=F32)
        + jnp.dot(weights[:, pl.ds(rows_txt, rows_txt)], panel_far, preferred_element_type=F32)
    ).reshape(n_z, 2, half_rows, width)

    def part_of(way, half, m):
        return cov_part[(-m if way == 0 else m) % n_z, half]

    def sum_copy(way, half, m):
        src = last_out.at[way, half] if m == 1 else rs_out.at[way, half, m - 1]
        dst = last_in.at[way, half] if m == 1 else rs_in.at[way, half, m - 1]
        return remote(
            src, dst,
            rs_send.at[way, half, m - 1], rs_recv.at[way, half, m - 1], z_next[way],
        )

    def sum_start(way, half, m):
        total = part_of(way, half, m)
        if m < hops(way, half):
            sum_copy(way, half, m + 1).wait_recv()
            total = total + rs_in[way, half, m].astype(F32)
        if m == 1:
            last_out[way, half] = total
        else:
            rs_out[way, half, m - 1] = total.astype(BF16)
        sum_copy(way, half, m).start()

    for half in range(2):
        for way in range(2):
            sum_start(way, half, hops(way, half))
    text_out[...] = text_term(0)

    def forward(j):
        for way in range(2):
            first_leg(way, j).wait_recv()
            second_leg(way, j).start()

    forwarded = 0
    for step in range(1, reach):
        for half in range(2):
            if forwarded < PIECES:
                forward(forwarded)
                forwarded += 1
            for way in range(2):
                m = hops(way, half) - step
                if m >= 1:
                    sum_start(way, half, m)
    for j in range(forwarded, PIECES):
        forward(j)

    for half in range(2):
        total = cov_part[0, half]
        for way in range(2):
            sum_copy(way, half, 1).wait_recv()
            total = total + last_in[way, half]
        cov_out[pl.ds(half * half_rows, half_rows)] = total

    for j in range(PIECES):
        for way in range(2):
            second_leg(way, j).wait_recv()
            rows = pl.ds((way * PIECES + j) * piece, piece)
            text_out[rows] = text_out[rows] + tx_in[way, j].astype(F32)

    lab_copy.wait_send()
    if TIE_RELAY:
        for way in range(2):
            tie_copy(way).wait_send()
            remote(tie_buf.at[way], tie_buf.at[way], tie_out.at[way], far_recv, far).wait_send()
    n_far = sections - (per_y if TIE_RELAY else 0)
    remote(text_ref.at[pl.ds(0, n_far)], panel.at[1, pl.ds(0, n_far)], far_send, far_recv, far).wait_send()
    n_near = sections - 1
    remote(text_ref.at[pl.ds(0, n_near)], panel.at[0, pl.ds(0, n_near)], near_send, near_recv, far).wait_send()
    for half in range(2):
        for way in range(2):
            for k in range(hops(way, half)):
                gather_copy(way, half, k).wait_send()
                sum_copy(way, half, k + 1).wait_send()
    for j in range(PIECES):
        for way in range(2):
            first_leg(way, j).wait_send()
            second_leg(way, j).wait_send()


def local(dims, text_emb, covariate, labels, logit_scale, logit_bias):
    n_z, y_lo, per_y = dims
    sections = y_lo * per_y
    cov_own = covariate[0]
    rows_dev, width = cov_own.shape
    rows_txt = labels.shape[1]
    piece = rows_txt // (2 * PIECES)
    reach = n_z // 2
    half_rows = rows_dev // 2
    dma = pltpu.SemaphoreType.DMA
    vmem = pl.BlockSpec(memory_space=pltpu.VMEM)
    smem = pl.BlockSpec(memory_space=pltpu.SMEM)
    text_grad, cov_grad = pl.pallas_call(
        functools.partial(kernel, dims),
        out_shape=(
            jax.ShapeDtypeStruct((rows_txt, width), F32),
            jax.ShapeDtypeStruct((rows_dev, width), F32),
        ),
        in_specs=[vmem, vmem, vmem, smem, smem],
        out_specs=(vmem, vmem),
        scratch_shapes=[
            pltpu.VMEM((2, sections, text_emb.shape[1], width), BF16),
            pltpu.VMEM((2, per_y // 2, text_emb.shape[1], width), BF16),
            pltpu.VMEM((n_z, 2, half_rows, width), BF16),
            pltpu.VMEM((1, rows_txt), jnp.int32),
            pltpu.VMEM((n_z * rows_dev, 2 * rows_txt), BF16),
            pltpu.VMEM((n_z, 2, half_rows, width), F32),
            pltpu.VMEM((2, 2, reach, half_rows, width), BF16),
            pltpu.VMEM((2, 2, reach, half_rows, width), BF16),
            pltpu.VMEM((2, 2, half_rows, width), F32),
            pltpu.VMEM((2, 2, half_rows, width), F32),
            pltpu.VMEM((2, PIECES, piece, width), BF16),
            pltpu.VMEM((2, PIECES, piece, width), BF16),
            pltpu.VMEM((2, PIECES, piece, width), BF16),
            dma((2, 2, reach)), dma((2, 2, reach)), dma((2, 2, reach)), dma((2, 2, reach)),
            dma((2, PIECES)), dma((2, PIECES)), dma((2, PIECES)), dma((2, PIECES)),
            dma((2,)), dma((2,)),
            dma((2,)), dma((2,)), dma((2,)), dma((2,)), dma((2,)),
        ],
        compiler_params=pltpu.CompilerParams(
            collective_id=0, has_side_effects=True, vmem_limit_bytes=48 * 1024 * 1024
        ),
    )(text_emb, cov_own, labels, logit_scale, logit_bias)
    return text_grad[None], cov_grad[None]


def solution(mesh):
    dims = (mesh.shape["blk"] // 2, Y_LO, mesh.shape["section"] // Y_LO)
    return jax.shard_map(
        functools.partial(local, dims),
        mesh=mesh,
        in_specs=(
            P(None, ("blk", "section"), None),
            P("section", "blk", None),
            P("section", "blk"),
            P(),
            P(),
        ),
        out_specs=(P("section", "blk", None), P("section", "blk", None)),
        check_vma=False,
    )
```
